32 devices in a mesh: grp: 2 (over y), seg: 4 (over z), tm: 2 (over x), rep: 2 (over core).
Axes of the slice: x: 2, y: 2, z: 4, core: 2. Of those that a mesh axis runs over, the one named last changes fastest.
Arguments:
- series: bfloat16 [3072, 2, 16, 128], P(('grp', 'seg'), 'rep', 'tm'), parts along dimension 0, may hold values from -6 to 6
- cotangent: bfloat16 [3072, 2, 16, 128], P(('grp', 'seg'), 'rep', 'tm'), parts along dimension 0, may hold values from -6 to 6
- w_filter: bfloat16 [2, 128, 128], replicated, may hold values from -0.375 to 0.375
- w_gate: bfloat16 [2, 128, 128], replicated, may hold values from -0.375 to 0.375
- b_filter: float32 [128], replicated, may hold values from -3 to 3
- b_gate: float32 [128], replicated, may hold values from -3 to 3
- w_diff: bfloat16 [3, 128, 128], replicated, may hold values from -0.5 to 0.5
- b_diff: float32 [128], replicated, may hold values from -3 to 3
- tile_row: int32 [8, 9], P(('grp', 'seg')), parts along dimension 0, may hold values from 0 to 2, as said below
- tile_col: int32 [8, 9], P(('grp', 'seg')), parts along dimension 0, may hold values from 0 to 5, as said below
- tile_val: bfloat16 [8, 9, 128, 128], P(('grp', 'seg')), parts along dimension 0, may hold values from -0.5 to 0.5
- send_nodes: int32 [8, 3, 128], P(('grp', 'seg')), parts along dimension 0, may hold values from 0 to 383
- send_count: int32 [8, 3], P(('grp', 'seg')), parts along dimension 0, may hold values from 0 to 128, as said below
Outputs:
- output: bfloat16 [3072, 2, 16, 128], P(('grp', 'seg'), 'rep', 'tm'), parts along dimension 0
- grad_series: bfloat16 [3072, 2, 16, 128], P(('grp', 'seg'), 'rep', 'tm'), parts along dimension 0
- grad_w_filter: float32 [4, 128, 128], P('grp'), parts along dimension 0
- grad_w_gate: float32 [4, 128, 128], P('grp'), parts along dimension 0
- grad_b_filter: float32 [256], P('grp'), parts along dimension 0
- grad_b_gate: float32 [256], P('grp'), parts along dimension 0
- grad_w_diff: float32 [6, 128, 128], P('grp'), parts along dimension 0
- grad_b_diff: float32 [256], P('grp'), parts along dimension 0
The draws below stay inside these ranges and needn't reach their ends.
There are 2 independent parts, one for each index of `grp`. The reference program is written for one: setup_inputs(seed, part) draws one part's arguments, and reference() takes and returns one part's arrays. A program takes and returns all parts, laid end to end along the dimension named above; an argument that names none is the same for every part. Nothing has to cross between parts.
Inputs may be any that keep to these rules, and one draw needn't show every extreme that they name: The first 3 tiles of each partition have tile_row 0, 1, ..., 2 in order. The first 3 tiles of each partition have tile_col 0, ..., 2 and the next 3 have tile_col 3, ..., 5, in order. `send_count`: list j of partition q is read by partition (q - d_j) mod 4; list 0 of every partition has 128 live entries.
All inputs are finite; a program needn't handle non-finite values.
Results may differ from the reference program's by a relative error of at most 0.0062.
Values may be sent and summed in bfloat16 or wider, within the bound.
A program may use at most 128 MiB of HBM per device.

```python
import math
import jax
import jax.numpy as jnp
from jax import lax

C = 128
TILE = 128
DILATION_FRAMES = 8
NODE_DEV = 384
NBR = 3
CAPN = 128
NB = 3
HALO = 384
HB = 3
NT = 9
NODES = 1536
WINDOW_FRAMES = 16
BATCH = 2
ROWS = 49152
N_SEG = 4


def draw_tile_row(key, part):
    diagonal = jnp.broadcast_to(jnp.arange(NB, dtype=jnp.int32)[None, :], (N_SEG, NB))
    extra_rows = jax.random.randint(key, (N_SEG, NT - NB), 0, NB, dtype=jnp.int32)
    return jnp.concatenate([diagonal, extra_rows], axis=1).astype(jnp.int32)


def draw_tile_col(key, part):
    diagonal = jnp.broadcast_to(jnp.arange(NB, dtype=jnp.int32)[None, :], (N_SEG, NB))
    boundary = jnp.broadcast_to(NB + jnp.arange(HB, dtype=jnp.int32)[None, :], (N_SEG, HB))
    extra_cols = jax.random.randint(key, (N_SEG, NT - NB - HB), 0, NB + HB, dtype=jnp.int32)
    return jnp.concatenate([diagonal, boundary, extra_cols], axis=1).astype(jnp.int32)


def draw_send_count(key, part):
    counts = jax.random.randint(key, (N_SEG, NBR), 0, CAPN + 1, dtype=jnp.int32)
    col_ids = lax.broadcasted_iota(jnp.int32, (N_SEG, NBR), 1)
    counts = jnp.where(col_ids == 0, CAPN, counts)
    return counts.astype(jnp.int32)


def plant(result, rng, low, top_value):
    dims = result.shape
    index_at = [jax.random.randint(jax.random.fold_in(rng, axis), (), 0, dims[axis]) for axis in range(len(dims))]
    result = result.at[tuple(index_at)].set(low)
    longest = dims.index(max(dims))
    index_at[longest] = (index_at[longest] + 1) % dims[longest]
    return result.at[tuple(index_at)].set(top_value)


def block_scale(stream_key, shape, cuts, low, high):
    factor_of, own = 1.0, jax.random.fold_in(stream_key, 6)
    for dim, parts in cuts:
        steps = jnp.exp(jax.random.uniform(jax.random.fold_in(own, dim), (parts,), jnp.float32, low / len(cuts), high / len(cuts)))
        factor_of = factor_of * jnp.repeat(steps, shape[dim] // parts).reshape([-1 if axis == dim else 1 for axis in range(len(shape))])
    return factor_of


def gaussian(stream_key, shape, scale, most, cuts=(), kind=jnp.bfloat16):
    factor_of = block_scale(stream_key, shape, cuts, -0.22, 0.18) if cuts else 1.0
    drawn = jax.random.normal(stream_key, shape, jnp.float32) * scale * factor_of
    return jnp.minimum(jnp.maximum(drawn, -most), most).astype(kind)


def setup_inputs(seed: int = 0, part: int = 0) -> dict:
    key_of = jax.random.split(jax.random.key(seed), 14)
    own_keys = jax.random.split(jax.random.fold_in(key_of[13], part), 14)
    series = gaussian(own_keys[0], (NODES, BATCH, WINDOW_FRAMES, C), 1.0, 6.0, ((0, 4), (1, 2), (2, 2)))
    cotangent = gaussian(own_keys[1], (NODES, BATCH, WINDOW_FRAMES, C), 1.0, 6.0, ((0, 4), (1, 2), (2, 2)))
    w_filter = gaussian(key_of[2], (2, C, C), (2 * C) ** -0.5, 0.375)
    w_gate = gaussian(key_of[3], (2, C, C), (2 * C) ** -0.5, 0.375)
    b_filter = gaussian(key_of[4], (C,), 0.5, 3.0, (), jnp.float32)
    b_gate = gaussian(key_of[5], (C,), 0.5, 3.0, (), jnp.float32)
    w_diff = gaussian(key_of[6], (3, C, C), C ** -0.5, 0.5)
    b_diff = gaussian(key_of[7], (C,), 0.5, 3.0, (), jnp.float32)
    tile_row = draw_tile_row(jax.random.fold_in(jax.random.fold_in(key_of[13], part), 71), part)
    tile_col = draw_tile_col(jax.random.fold_in(jax.random.fold_in(key_of[13], part), 71), part)
    tile_val = gaussian(own_keys[10], (N_SEG, NT, TILE, TILE), TILE ** -0.5, 0.5, ((0, 4),))
    send_nodes = plant(jax.random.randint(own_keys[11], (N_SEG, NBR, CAPN), 0, NODE_DEV), jax.random.fold_in(own_keys[11], 1), 0, NODE_DEV - 1).astype(jnp.int32)
    send_count = draw_send_count(jax.random.fold_in(jax.random.fold_in(key_of[13], part), 71), part)
    return {"series": series, "cotangent": cotangent, "w_filter": w_filter, "w_gate": w_gate, "b_filter": b_filter, "b_gate": b_gate, "w_diff": w_diff, "b_diff": b_diff, "tile_row": tile_row, "tile_col": tile_col, "tile_val": tile_val, "send_nodes": send_nodes, "send_count": send_count}


neighbour_steps = (1, -1, 2)

def linear_map(inputs, weight):
    return jnp.dot(inputs, weight, preferred_element_type=jnp.float32)

def linear_back(inputs, weight):
    return lax.dot_general(inputs, weight, (((1,), (1,)), ((), ())), preferred_element_type=jnp.float32)

def outer_sum(left_rows, right_rows):
    return lax.dot_general(left_rows, right_rows, (((0,), (0,)), ((), ())), preferred_element_type=jnp.float32)

def pre_acts(prior_frames, current, w_filter, w_gate, b_filter, b_gate):
    channels = current.shape[-1]
    prev_rows = prior_frames.reshape(-1, channels)
    curr_rows = current.reshape(-1, channels)
    filter_pre = linear_map(prev_rows, w_filter[0]) + linear_map(curr_rows, w_filter[1]) + b_filter
    gate_pre = linear_map(prev_rows, w_gate[0]) + linear_map(curr_rows, w_gate[1]) + b_gate
    return (filter_pre, gate_pre)

def gated_units(filter_pre, gate_pre):
    return (jnp.tanh(filter_pre) * jax.nn.sigmoid(gate_pre)).astype(jnp.bfloat16)

def spread_tiles(source, row_list, col_list, tile_values, out_rows):
    tile_side = tile_values.shape[1]
    row_width = source.shape[1]

    def add_tile(tile_index, running):
        source_piece = lax.dynamic_slice_in_dim(source, col_list[tile_index] * tile_side, tile_side, 0)
        product = jnp.dot(tile_values[tile_index], source_piece, preferred_element_type=jnp.float32)
        row_start = row_list[tile_index] * tile_side
        current = lax.dynamic_slice_in_dim(running, row_start, tile_side, 0)
        return lax.dynamic_update_slice_in_dim(running, current + product, row_start, 0)
    return lax.fori_loop(0, tile_values.shape[0], add_tile, jnp.zeros((out_rows, row_width), jnp.float32))

def gather_tiles(cotan, row_list, col_list, tile_values, out_rows):
    tile_side = tile_values.shape[1]
    row_width = cotan.shape[1]

    def add_tile(tile_index, running):
        source_piece = lax.dynamic_slice_in_dim(cotan, row_list[tile_index] * tile_side, tile_side, 0)
        product = outer_sum(tile_values[tile_index], source_piece)
        row_start = col_list[tile_index] * tile_side
        current = lax.dynamic_slice_in_dim(running, row_start, tile_side, 0)
        return lax.dynamic_update_slice_in_dim(running, current + product, row_start, 0)
    return lax.fori_loop(0, tile_values.shape[0], add_tile, jnp.zeros((out_rows, row_width), jnp.float32))

def reference(series, cotangent, w_filter, w_gate, b_filter, b_gate, w_diff, b_diff, tile_row, tile_col, tile_val, send_nodes, send_count):
    row_width = BATCH * WINDOW_FRAMES * C
    prior_frames = jnp.pad(series, ((0, 0), (0, 0), (DILATION_FRAMES, 0), (0, 0)))[:, :, :WINDOW_FRAMES]
    filter_pre, gate_pre = pre_acts(prior_frames, series, w_filter, w_gate, b_filter, b_gate)
    hidden = gated_units(filter_pre, gate_pre)
    live_slots = jnp.arange(CAPN, dtype=jnp.int32)[None, None, :] < send_count[:, :, None]
    owners = jnp.arange(N_SEG, dtype=jnp.int32)

    def forward_op(field):
        blocks = field.reshape(N_SEG, NODE_DEV, row_width)

        def one_part(part_id):
            pieces = [blocks[part_id]]
            for neighbour, offset in enumerate(neighbour_steps):
                owner = ((part_id + offset) % N_SEG).astype(jnp.int32)
                picked = blocks[owner][send_nodes[owner, neighbour]]
                picked = jnp.where(live_slots[owner, neighbour][:, None], picked, jnp.zeros((), field.dtype))
                pieces.append(picked)
            source = jnp.concatenate(pieces, axis=0)
            return spread_tiles(source, tile_row[part_id], tile_col[part_id], tile_val[part_id], NODE_DEV)
        return lax.map(one_part, owners).reshape(NODES, row_width)

    def backward_op(cotan):
        blocks = cotan.reshape(N_SEG, NODE_DEV, row_width)

        def one_part(part_id):
            summed = gather_tiles(blocks[part_id], tile_row[part_id], tile_col[part_id], tile_val[part_id], NODE_DEV + HALO)
            return (summed[:NODE_DEV], summed[NODE_DEV:].astype(jnp.bfloat16))
        local_part, halo_part = lax.map(one_part, owners)
        halo_part = halo_part.reshape(N_SEG, NBR, CAPN, row_width)

        def one_owner(owner_id):
            total = jnp.zeros((NODE_DEV, row_width), jnp.float32)
            for neighbour, offset in enumerate(neighbour_steps):
                reader = ((owner_id - offset) % N_SEG).astype(jnp.int32)
                incoming = halo_part[reader, neighbour].astype(jnp.float32)
                incoming = incoming * live_slots[owner_id, neighbour][:, None].astype(jnp.float32)
                total = total.at[send_nodes[owner_id, neighbour]].add(incoming)
            return total
        scattered = lax.map(one_owner, owners)
        return (local_part + scattered).reshape(NODES, row_width)
    hop_one = forward_op(hidden.reshape(NODES, row_width)).astype(jnp.bfloat16)
    hop_two = forward_op(hop_one).astype(jnp.bfloat16)
    one_rows = hop_one.reshape(-1, C)
    two_rows = hop_two.reshape(-1, C)
    diffusion_out = linear_map(hidden, w_diff[0]) + linear_map(one_rows, w_diff[1]) + linear_map(two_rows, w_diff[2]) + b_diff
    output = (series.reshape(-1, C).astype(jnp.float32) + diffusion_out).astype(jnp.bfloat16).reshape(series.shape)
    grad_scale = 1.0 / math.sqrt(ROWS)
    grad_rows = cotangent.reshape(-1, C)
    grad_b_diff = lax.optimization_barrier(jnp.sum(grad_rows.astype(jnp.float32), axis=0)) * grad_scale
    grad_w_diff = jnp.stack([outer_sum(hidden, grad_rows), outer_sum(one_rows, grad_rows), outer_sum(two_rows, grad_rows)]) * grad_scale
    up_two = linear_back(grad_rows, w_diff[2]).astype(jnp.bfloat16)
    up_one = (linear_back(grad_rows, w_diff[1]) + backward_op(up_two.reshape(NODES, row_width)).reshape(-1, C)).astype(jnp.bfloat16)
    grad_hidden = linear_back(grad_rows, w_diff[0]) + backward_op(up_one.reshape(NODES, row_width)).reshape(-1, C)
    act_filter = jnp.tanh(filter_pre)
    act_gate = jax.nn.sigmoid(gate_pre)
    grad_filter = (grad_hidden * act_gate * (1.0 - act_filter * act_filter)).astype(jnp.bfloat16)
    grad_gate = (grad_hidden * act_filter * (act_gate * (1.0 - act_gate))).astype(jnp.bfloat16)
    prev_rows = prior_frames.reshape(-1, C)
    curr_rows = series.reshape(-1, C)
    grad_w_filter = jnp.stack([outer_sum(prev_rows, grad_filter), outer_sum(curr_rows, grad_filter)]) * grad_scale
    grad_b_filter = lax.optimization_barrier(jnp.sum(grad_filter.astype(jnp.float32), axis=0)) * grad_scale
    grad_w_gate = jnp.stack([outer_sum(prev_rows, grad_gate), outer_sum(curr_rows, grad_gate)]) * grad_scale
    grad_b_gate = lax.optimization_barrier(jnp.sum(grad_gate.astype(jnp.float32), axis=0)) * grad_scale
    lagged_series = (linear_back(grad_filter, w_filter[0]) + linear_back(grad_gate, w_gate[0])).astype(jnp.bfloat16)
    lagged_series = lagged_series.reshape(series.shape)
    forward_moved = jnp.pad(lagged_series, ((0, 0), (0, 0), (0, DILATION_FRAMES), (0, 0)))[:, :, DILATION_FRAMES:]
    grad_series = (grad_rows.astype(jnp.float32) + linear_back(grad_filter, w_filter[1]) + linear_back(grad_gate, w_gate[1]) + forward_moved.reshape(-1, C).astype(jnp.float32)).astype(jnp.bfloat16).reshape(series.shape)
    return (output, grad_series, grad_w_filter, grad_w_gate, grad_b_filter, grad_b_gate, grad_w_diff, grad_b_diff)
```

```python
import functools
import math

import jax
import jax.numpy as jnp
from jax import lax
from jax.experimental import pallas as pl
from jax.experimental.pallas import tpu as pltpu
from jax.sharding import PartitionSpec as P

DILATION_FRAMES = 8
STEPS = (1, -1, 2)
MESH = pl.DeviceIdType.MESH
WIDE = 256
BF = jnp.bfloat16
F32 = jnp.float32


def mm(a, b):
    return lax.dot_general(a, b, (((1,), (0,)), ((), ())), preferred_element_type=F32)


def mm_nt(a, b):
    return lax.dot_general(a, b, (((1,), (1,)), ((), ())), preferred_element_type=F32)


def mm_tn(a, b):
    return lax.dot_general(a, b, (((0,), (0,)), ((), ())), preferred_element_type=F32)


def kernel(
    seg_n, tm_n, scale,
    ser, cot, wf, wg, bf, bg, wd, bd, trow, tcol, tval, snodes, scount,
    out, gs, fin1, fin2,
    prev, ops_f, ops_b, pick, give, wblk,
    acc, act_f, act_g, hid, hop1, delayed_out, delayed_in,
    snd, rcv, wacc, dacc, bacc, cacc,
    red1, red2, ra1, rb1, rc1, sa1, sb1, ra2, rb2, rc2, sa2, sb2,
    tm_s, tm_r, ex_s, ex_r, dl_s, dl_r, ar_s, ar_r,
):
    p = lax.axis_index("seg")
    t = lax.axis_index("tm")
    rep = lax.axis_index("rep")
    chunks, nodes, _ = ser.shape
    cap = 128
    ch = 128

    barrier = pltpu.get_barrier_semaphore()
    for k in range(1, seg_n):
        pl.semaphore_signal(barrier, inc=1, device_id={"seg": lax.rem(p + k, seg_n)}, device_id_type=MESH)
    for k in range(1, tm_n):
        pl.semaphore_signal(barrier, inc=1, device_id={"tm": lax.rem(t + k, tm_n)}, device_id_type=MESH)
    pl.semaphore_signal(barrier, inc=1, device_id={"rep": 1 - rep}, device_id_type=MESH)
    pl.semaphore_wait(barrier, seg_n - 1 + tm_n - 1 + 1)

    def series_copy(c):
        return pltpu.make_async_remote_copy(
            src_ref=ser.at[c], dst_ref=prev.at[c], send_sem=tm_s.at[c], recv_sem=tm_r.at[c],
            device_id={"tm": lax.rem(t + 1, tm_n)}, device_id_type=MESH)

    def delayed_copy(c):
        return pltpu.make_async_remote_copy(
            src_ref=delayed_out.at[c], dst_ref=delayed_in.at[c], send_sem=dl_s.at[c], recv_sem=dl_r.at[c],
            device_id={"tm": lax.rem(t + tm_n - 1, tm_n)}, device_id_type=MESH)

    def halo_copy(e, c, j):
        step = STEPS[j] if e % 2 == 0 else -STEPS[j]
        return pltpu.make_async_remote_copy(
            src_ref=snd.at[e, c, j], dst_ref=rcv.at[e, c, j],
            send_sem=ex_s.at[e, c, j], recv_sem=ex_r.at[e, c, j],
            device_id={"seg": lax.rem(p + step + seg_n, seg_n)}, device_id_type=MESH)

    @pl.when(t < tm_n - 1)
    def _():
        for c in range(chunks):
            series_copy(c).start()

    @pl.when(t == 0)
    def _():
        prev[...] = jnp.zeros_like(prev)

    rows_n, cols_n, tiles_n = nodes // 128, nodes // 128 + 3, tval.shape[0]
    for r in range(rows_n):
        for c in range(cols_n):
            total = jnp.zeros((128, 128), F32)
            for k in range(tiles_n):
                if k < rows_n and (r != k or c != k):
                    continue
                if rows_n <= k < cols_n and c != k:
                    continue
                hit = jnp.where(trow[0, k] == r, 1.0, 0.0) * jnp.where(tcol[0, k] == c, 1.0, 0.0)
                total = total + hit * tval[k].astype(F32)
            ops_f[r * 128:(r + 1) * 128, c * 128:(c + 1) * 128] = total.astype(BF)
            ops_b[c * 128:(c + 1) * 128, r * 128:(r + 1) * 128] = total.T.astype(BF)
    node_ids = lax.broadcasted_iota(jnp.int32, (nodes, cap), 0)
    slot_ids = lax.broadcasted_iota(jnp.int32, (nodes, cap), 1)
    for j in range(3):
        here = jnp.where(node_ids == snodes[j:j + 1, :], 1.0, 0.0)
        live = jnp.where(slot_ids < scount[0, j], 1.0, 0.0)
        hot = here * live
        give[:, j * cap:(j + 1) * cap] = hot.astype(BF)
        pick[j * cap:(j + 1) * cap, :] = hot.T.astype(BF)
    wblk[...] = jnp.zeros_like(wblk)
    for i in range(2):
        lo, hi = i * ch, (i + 1) * ch
        for k in range(2):
            wblk[k, lo:hi, lo:hi] = wf[k]
            wblk[2 + k, lo:hi, lo:hi] = wg[k]
        for k in range(3):
            wblk[4 + k, lo:hi, lo:hi] = wd[k]
    wacc[...] = jnp.zeros_like(wacc)
    dacc[...] = jnp.zeros_like(dacc)
    bacc[...] = jnp.zeros_like(bacc)
    cacc[...] = jnp.zeros_like(cacc)
    red1[...] = jnp.zeros_like(red1)
    red2[...] = jnp.zeros_like(red2)
    ones = jnp.ones((8, nodes), BF)

    def put(e, c, rows):
        for j in range(3):
            snd[e, c, j] = rows[j * cap:(j + 1) * cap]
            halo_copy(e, c, j).start()

    def back_one(c, _):
        g = cot[c]
        up = mm_nt(g, wblk[6]).astype(BF)
        put(0, c, mm(ops_b[nodes:, :], up).astype(BF))
        acc[c] = mm(ops_b[:nodes, :], up) + mm_nt(g, wblk[5])
        return 0

    lax.fori_loop(0, chunks, back_one, 0)

    bf2 = jnp.concatenate([bf[...], bf[...]], axis=1)
    bg2 = jnp.concatenate([bg[...], bg[...]], axis=1)
    bd2 = jnp.concatenate([bd[...], bd[...]], axis=1)

    def fore_one(c, _):
        @pl.when(t > 0)
        def _():
            series_copy(c).wait_recv()

        before, now = prev[c], ser[c]
        a = jnp.tanh(mm(before, wblk[0]) + mm(now, wblk[1]) + bf2)
        act_f[c] = a
        s = jax.nn.sigmoid(mm(before, wblk[2]) + mm(now, wblk[3]) + bg2)
        act_g[c] = s
        h = (a * s).astype(BF)
        hid[c] = h
        put(1, c, mm(pick[...], h).astype(BF))
        return 0

    lax.fori_loop(0, chunks, fore_one, 0)

    def arrived(e, c):
        for j in range(3):
            halo_copy(e, c, j).wait_recv()
        return rcv[e, c].reshape(3 * cap, WIDE)

    def back_two(c, _):
        got = arrived(0, c)
        up = (acc[c] + mm(give[...], got)).astype(BF)
        put(2, c, mm(ops_b[nodes:, :], up).astype(BF))
        acc[c] = mm(ops_b[:nodes, :], up) + mm_nt(cot[c], wblk[4])
        return 0

    lax.fori_loop(0, chunks, back_two, 0)

    def fore_two(c, _):
        got = arrived(1, c)
        h = (mm(ops_f[:, :nodes], hid[c]) + mm(ops_f[:, nodes:], got)).astype(BF)
        hop1[c] = h
        put(3, c, mm(pick[...], h).astype(BF))
        return 0

    lax.fori_loop(0, chunks, fore_two, 0)

    def back_three(c, _):
        got = arrived(2, c)
        gh = acc[c] + mm(give[...], got)
        a, s = act_f[c], act_g[c]
        gf = (gh * s * (1.0 - a * a)).astype(BF)
        gg = (gh * a * (s * (1.0 - s))).astype(BF)
        delayed_out[c] = (mm_nt(gf, wblk[0]) + mm_nt(gg, wblk[2])).astype(BF)

        @pl.when(t > 0)
        def _():
            delayed_copy(c).start()

        g = cot[c]
        acc[c] = g.astype(F32) + mm_nt(gf, wblk[1]) + mm_nt(gg, wblk[3])
        before, now, h, h1 = prev[c], ser[c], hid[c], hop1[c]
        for i in range(2):
            lo, hi = i * ch, (i + 1) * ch
            right = jnp.concatenate([gf[:, lo:hi], gg[:, lo:hi]], axis=1)
            left = jnp.concatenate([before[:, lo:hi], now[:, lo:hi]], axis=1)
            wacc[...] += mm_tn(left, right)
            dacc[...] += mm_tn(jnp.concatenate([h[:, lo:hi], h1[:, lo:hi]], axis=1), g[:, lo:hi])
            bacc[...] += mm(ones, right)
            cacc[...] += mm(ones, g[:, lo:hi])
        return 0

    lax.fori_loop(0, chunks, back_three, 0)

    red1[0:256, :] = wacc[:, 0:128]
    red1[256:512, :] = wacc[:, 128:256]
    red1[512:768, :] = dacc[...]
    rid = lax.broadcasted_iota(jnp.int32, (8, 128), 0)
    red1[768:776, :] = jnp.where(
        rid == 0, bacc[:, 0:128], jnp.where(rid == 1, bacc[:, 128:256], cacc[...]))

    def all_sum(base, red, ra, rb, rc, sa, sb, fin):
        half = red.shape[0] // 2
        part = half // tm_n
        mine = pl.multiple_of(rep * half, 8)
        theirs = pl.multiple_of((1 - rep) * half, 8)
        one = pltpu.make_async_remote_copy(
            src_ref=red.at[pl.ds(theirs, half)], dst_ref=ra,
            send_sem=ar_s.at[base], recv_sem=ar_r.at[base],
            device_id={"rep": 1 - rep}, device_id_type=MESH)
        one.start()
        one.wait()
        sa[...] = red[pl.ds(mine, half), :] + ra[...]
        sends = []
        for k in range(1, tm_n):
            o = lax.rem(t + k, tm_n)
            sends.append(pltpu.make_async_remote_copy(
                src_ref=sa.at[pl.ds(pl.multiple_of(o * part, 8), part)], dst_ref=rb.at[k - 1],
                send_sem=ar_s.at[base + k], recv_sem=ar_r.at[base + k],
                device_id={"tm": o}, device_id_type=MESH))
            sends[-1].start()
        s = sa[pl.ds(pl.multiple_of(t * part, 8), part), :]
        for k in range(1, tm_n):
            sends[k - 1].wait()
            s = s + rb[k - 1]
        sb[...] = s
        rc[p] = s
        at = base + tm_n
        sends = []
        for k in range(1, seg_n):
            sends.append(pltpu.make_async_remote_copy(
                src_ref=sb, dst_ref=rc.at[p],
                send_sem=ar_s.at[at + k], recv_sem=ar_r.at[at + k],
                device_id={"seg": lax.rem(p + k, seg_n)}, device_id_type=MESH))
            sends[-1].start()
        for copy in sends:
            copy.wait()
        s = rc[0]
        for k in range(1, seg_n):
            s = s + rc[k]
        spot = pl.multiple_of(rep * half + t * part, 8)
        fin[pl.ds(spot, part), :] = s * scale
        at = at + seg_n
        sends = []
        for k in range(1, tm_n):
            sends.append(pltpu.make_async_remote_copy(
                src_ref=fin.at[pl.ds(spot, part)], dst_ref=fin.at[pl.ds(spot, part)],
                send_sem=ar_s.at[at + k], recv_sem=ar_r.at[at + k],
                device_id={"tm": lax.rem(t + k, tm_n)}, device_id_type=MESH))
            sends[-1].start()
        for copy in sends:
            copy.wait()
        at = at + tm_n
        last = pltpu.make_async_remote_copy(
            src_ref=fin.at[pl.ds(mine, half)], dst_ref=fin.at[pl.ds(mine, half)],
            send_sem=ar_s.at[at], recv_sem=ar_r.at[at],
            device_id={"rep": 1 - rep}, device_id_type=MESH)
        last.start()
        last.wait()

    all_sum(0, red1, ra1, rb1, rc1, sa1, sb1, fin1)

    def fore_three(c, _):
        got = arrived(3, c)
        h, h1, g = hid[c], hop1[c], cot[c]
        h2 = (mm(ops_f[:, :nodes], h1) + mm(ops_f[:, nodes:], got)).astype(BF)
        total = mm(h, wblk[4]) + mm(h1, wblk[5]) + mm(h2, wblk[6]) + bd2
        out[c] = (ser[c].astype(F32) + total).astype(BF)
        for i in range(2):
            lo, hi = i * ch, (i + 1) * ch
            red2[...] += mm_tn(h2[:, lo:hi], g[:, lo:hi])
        return 0

    lax.fori_loop(0, chunks, fore_three, 0)

    def series_grad(c, _):
        @pl.when(t < tm_n - 1)
        def _():
            delayed_copy(c).wait_recv()
            gs[c] = (acc[c] + delayed_in[c].astype(F32)).astype(BF)

        @pl.when(t == tm_n - 1)
        def _():
            gs[c] = acc[c].astype(BF)

        return 0

    lax.fori_loop(0, chunks, series_grad, 0)
    all_sum(2 * tm_n + seg_n + 1, red2, ra2, rb2, rc2, sa2, sb2, fin2)

    def drain(c, _):
        @pl.when(t < tm_n - 1)
        def _():
            series_copy(c).wait_send()

        @pl.when(t > 0)
        def _():
            delayed_copy(c).wait_send()

        for e in range(4):
            for j in range(3):
                halo_copy(e, c, j).wait_send()
        return 0

    lax.fori_loop(0, chunks, drain, 0)


def on_device(mesh, series, cotangent, w_filter, w_gate, b_filter, b_gate, w_diff, b_diff,
              tile_row, tile_col, tile_val, send_nodes, send_count):
    nodes, batch, frames, channels = series.shape
    seg_n, tm_n, rep_n = mesh.shape["seg"], mesh.shape["tm"], mesh.shape["rep"]
    chunks = batch * frames * channels // WIDE
    scale = 1.0 / math.sqrt(nodes * batch * frames * seg_n * tm_n * rep_n)
    unit = 16 * tm_n
    r1 = -(-776 // unit) * unit
    r2 = -(-128 // unit) * unit

    def chunked(x):
        return x.reshape(nodes, chunks, WIDE).transpose(1, 0, 2)

    def whole(x):
        return x.transpose(1, 0, 2).reshape(nodes, batch, frames, channels)

    vmem = pl.BlockSpec(memory_space=pltpu.VMEM)
    smem = pl.BlockSpec(memory_space=pltpu.SMEM)
    field = (chunks, nodes, WIDE)

    def sums(r):
        h = r // 2
        q = h // tm_n
        return [
            pltpu.VMEM((h, 128), F32),
            pltpu.VMEM((max(tm_n - 1, 1), q, 128), F32),
            pltpu.VMEM((seg_n, q, 128), F32),
            pltpu.VMEM((h, 128), F32),
            pltpu.VMEM((q, 128), F32),
        ]

    n_ar = 2 * (2 * tm_n + seg_n + 1)
    halo = (4, chunks, 3, 128, WIDE)
    out, gs, fin1, fin2 = pl.pallas_call(
        functools.partial(kernel, seg_n, tm_n, scale),
        out_shape=(
            jax.ShapeDtypeStruct(field, BF),
            jax.ShapeDtypeStruct(field, BF),
            jax.ShapeDtypeStruct((r1, 128), F32),
            jax.ShapeDtypeStruct((r2, 128), F32),
        ),
        in_specs=[vmem] * 8 + [smem, smem, vmem, vmem, smem],
        out_specs=(vmem,) * 4,
        scratch_shapes=[
            pltpu.VMEM(field, BF),
            pltpu.VMEM((nodes, nodes + 384), BF),
            pltpu.VMEM((nodes + 384, nodes), BF),
            pltpu.VMEM((384, nodes), BF),
            pltpu.VMEM((nodes, 384), BF),
            pltpu.VMEM((7, WIDE, WIDE), BF),
            pltpu.VMEM(field, F32),
            pltpu.VMEM(field, F32),
            pltpu.VMEM(field, F32),
            pltpu.VMEM(field, BF),
            pltpu.VMEM(field, BF),
            pltpu.VMEM(field, BF),
            pltpu.VMEM(field, BF),
            pltpu.VMEM(halo, BF),
            pltpu.VMEM(halo, BF),
            pltpu.VMEM((256, 256), F32),
            pltpu.VMEM((256, 128), F32),
            pltpu.VMEM((8, 256), F32),
            pltpu.VMEM((8, 128), F32),
            pltpu.VMEM((r1, 128), F32),
            pltpu.VMEM((r2, 128), F32),
            *sums(r1),
            *sums(r2),
            pltpu.SemaphoreType.DMA((chunks,)),
            pltpu.SemaphoreType.DMA((chunks,)),
            pltpu.SemaphoreType.DMA((4, chunks, 3)),
            pltpu.SemaphoreType.DMA((4, chunks, 3)),
            pltpu.SemaphoreType.DMA((chunks,)),
            pltpu.SemaphoreType.DMA((chunks,)),
            pltpu.SemaphoreType.DMA((n_ar,)),
            pltpu.SemaphoreType.DMA((n_ar,)),
        ],
        compiler_params=pltpu.CompilerParams(
            collective_id=0, has_side_effects=True, vmem_limit_bytes=56 << 20),
    )(
        chunked(series), chunked(cotangent), w_filter, w_gate,
        b_filter.reshape(1, -1), b_gate.reshape(1, -1), w_diff, b_diff.reshape(1, -1),
        tile_row, tile_col, tile_val[0], send_nodes[0], send_count,
    )
    return (
        whole(out),
        whole(gs),
        fin1[0:256].reshape(2, 128, 128),
        fin1[256:512].reshape(2, 128, 128),
        fin1[768],
        fin1[769],
        jnp.concatenate([fin1[512:768], fin2[:128]], axis=0).reshape(3, 128, 128),
        fin1[770],
    )


def solution(mesh):
    field = P(("grp", "seg"), "rep", "tm", None)
    part = ("grp", "seg")
    in_specs = (
        field, field, P(), P(), P(), P(), P(), P(),
        P(part, None), P(part, None), P(part, None, None, None), P(part, None, None), P(part, None),
    )
    out_specs = (
        field, field, P("grp", None, None), P("grp", None, None), P("grp"), P("grp"),
        P("grp", None, None), P("grp"),
    )
    return jax.shard_map(
        functools.partial(on_device, mesh), mesh=mesh, in_specs=in_specs, out_specs=out_specs,
        check_vma=False)
```
